32 devices in a mesh: slab: 4 (over z), tile: 8 (over y, x, core).
Axes of the slice: x: 2, y: 2, z: 4, core: 2. Of those that a mesh axis runs over, the one named last changes fastest.
Arguments:
- coarse: bfloat16 [192, 16, 32, 64], P(None, 'slab', 'tile'), may hold values from -6 to 6
- up_weight: bfloat16 [3, 3, 96, 192], replicated, may hold values from -0.15625 to 0.15625
- up_bias: float32 [96], replicated, may hold values from -3 to 3
- gain_one: float32 [96], replicated, may hold values from 0.1 to 1.9
- conv_one: bfloat16 [3, 3, 96, 288], replicated, may hold values from -0.125 to 0.125
- bias_one: float32 [96], replicated, may hold values from -3 to 3
- gain_two: float32 [96], replicated, may hold values from 0.1 to 1.9
- conv_two: bfloat16 [3, 3, 96, 288], replicated, may hold values from -0.125 to 0.125
- bias_two: float32 [96], replicated, may hold values from -3 to 3
Outputs:
- decoded: bfloat16 [96, 16, 64, 128], P(None, 'slab', 'tile')
The draws below stay inside these ranges and needn't reach their ends.
All inputs are finite; a program needn't handle non-finite values.
Results may differ from the reference program's by a relative error of at most 0.009.
Values may be sent and summed in bfloat16 or wider, within the bound.
A program may use at most 64 MiB of HBM per device.

```python
import jax
import jax.numpy as jnp
from jax import lax

COARSE_CH = 192
FINE_CH = 96
COLS = 128
FRAMES = 16
ROWS = 64


def steps_of(key, dims, shards, low, largest):
    def one(dim, shards_of):
        heights = jax.random.uniform(jax.random.fold_in(jax.random.fold_in(key, 6), dim), (shards_of,), jnp.float32, low / len(shards), largest / len(shards))
        return jnp.repeat(jnp.exp(heights), dims[dim] // shards_of).reshape((-1,) + (1,) * (len(dims) - dim - 1))

    loudness = one(*shards[0])
    for cut in shards[1:]:
        loudness = loudness * one(*cut)
    return loudness


def bell_draw(stream_key, shape, width, limit, pieces=(), dtype=jnp.bfloat16):
    values = width * jax.random.normal(stream_key, shape, jnp.float32)
    if pieces:
        values = values * steps_of(stream_key, shape, pieces, -0.22, 0.18)
    return jnp.clip(values, -limit, limit).astype(dtype)


def setup_inputs(seed: int = 0) -> dict:
    arg_keys = jax.random.split(jax.random.key(seed), 10)
    coarse = bell_draw(arg_keys[0], (COARSE_CH, FRAMES, ROWS // 2, COLS // 2), 1.0, 6.0, ((1, 4), (2, 8)))
    up_weight = bell_draw(arg_keys[1], (3, 3, FINE_CH, COARSE_CH), (9 * COARSE_CH) ** -0.5, 0.15625)
    up_bias = bell_draw(arg_keys[2], (FINE_CH,), 0.5, 3.0, (), jnp.float32)
    gain_one = jnp.clip(1.0 + 0.18 * jax.random.normal(arg_keys[3], (FINE_CH,), jnp.float32), 0.1, 1.9)
    conv_one = bell_draw(arg_keys[4], (3, 3, FINE_CH, 3 * FINE_CH), (27 * FINE_CH) ** -0.5, 0.125)
    bias_one = bell_draw(arg_keys[5], (FINE_CH,), 0.5, 3.0, (), jnp.float32)
    gain_two = jnp.clip(1.0 + 0.18 * jax.random.normal(arg_keys[6], (FINE_CH,), jnp.float32), 0.1, 1.9)
    conv_two = bell_draw(arg_keys[7], (3, 3, FINE_CH, 3 * FINE_CH), (27 * FINE_CH) ** -0.5, 0.125)
    bias_two = bell_draw(arg_keys[8], (FINE_CH,), 0.5, 3.0, (), jnp.float32)
    return {"coarse": coarse, "up_weight": up_weight, "up_bias": up_bias, "gain_one": gain_one, "conv_one": conv_one, "bias_one": bias_one, "gain_two": gain_two, "conv_two": conv_two, "bias_two": bias_two}


def norm_act(values, gain):
    meansq = lax.optimization_barrier(jnp.mean(values * values, axis=0, keepdims=True))
    scaled = values * lax.rsqrt(meansq + 1e-06) * gain[:, None, None, None]
    return (scaled * jax.nn.sigmoid(scaled)).astype(jnp.bfloat16)

def conv_frame(window, weight, bias):
    chans = window.shape[0]
    padded = jnp.pad(window, ((0, 0), (0, 0), (1, 1), (1, 1)))
    height = padded.shape[2] - 2
    breadth = padded.shape[3] - 2
    summed = jnp.zeros((weight.shape[2], height * breadth), jnp.float32)
    for t_tap in range(3):
        for h_tap in range(3):
            stacked = jnp.concatenate([padded[:, t_tap, h_tap:h_tap + height, w_tap:w_tap + breadth] for w_tap in range(3)], axis=0)
            summed = summed + jnp.dot(weight[t_tap, h_tap], stacked.reshape(3 * chans, -1), preferred_element_type=jnp.float32)
    return summed.reshape(-1, 1, height, breadth) + bias[:, None, None, None]

def plane_frame(padded, weight, bias):
    chans = padded.shape[0]
    height = padded.shape[1] - 2
    breadth = padded.shape[2] - 2
    summed = jnp.zeros((weight.shape[2], height * breadth), jnp.float32)
    for h_tap in range(3):
        for w_tap in range(3):
            window = padded[:, h_tap:h_tap + height, w_tap:w_tap + breadth].reshape(chans, -1)
            summed = summed + jnp.dot(weight[h_tap, w_tap], window, preferred_element_type=jnp.float32)
    return summed.reshape(-1, 1, height, breadth) + bias[:, None, None, None]

def reference(coarse, up_weight, up_bias, gain_one, conv_one, bias_one, gain_two, conv_two, bias_two):
    chans = up_weight.shape[2]
    height = coarse.shape[2] * 2
    breadth = coarse.shape[3] * 2
    frames_first = jnp.moveaxis(coarse, 1, 0)

    def advance(carry, frame):
        past_one, past_two = carry
        enlarged = jnp.repeat(jnp.repeat(frame, 2, axis=1), 2, axis=2)
        enlarged = jnp.pad(enlarged, ((0, 0), (1, 1), (1, 1)))
        upsampled = plane_frame(enlarged, up_weight, up_bias).astype(jnp.bfloat16)
        first_act = norm_act(upsampled.astype(jnp.float32), gain_one)
        window_one = jnp.concatenate([past_one, first_act], axis=1)
        hidden = conv_frame(window_one, conv_one, bias_one)
        second_act = norm_act(hidden, gain_two)
        window_two = jnp.concatenate([past_two, second_act], axis=1)
        result = upsampled.astype(jnp.float32) + conv_frame(window_two, conv_two, bias_two)
        return ((window_one[:, 1:], window_two[:, 1:]), result[:, 0].astype(jnp.bfloat16))
    start = (jnp.zeros((chans, 2, height, breadth), jnp.bfloat16), jnp.zeros((chans, 2, height, breadth), jnp.bfloat16))
    final, outputs = lax.scan(advance, start, frames_first)
    return jnp.moveaxis(outputs, 0, 1)
```

```python
import functools

import jax
import jax.numpy as jnp
from jax import lax
from jax.experimental import pallas as pl
from jax.experimental.pallas import tpu as pltpu
from jax.sharding import PartitionSpec as P

MESH = pl.DeviceIdType.MESH
F32 = jnp.float32
BF16 = jnp.bfloat16


def body(slabs, tiles, coarse, wu, w1, w2, vecs, out, cbuf, part, ups, x1, acc1, x2, acc2,
         near_send, near_recv, far_send, far_recv, hop_send, hop_recv):
    frames, _, _, cols = coarse.shape
    chans = out.shape[2]
    rows = out.shape[1]
    s = lax.axis_index("slab")
    t = lax.axis_index("tile")
    has_up, has_down = t > 0, t < tiles - 1
    has_prev, has_next = s > 0, s < slabs - 1
    sides = ((has_up, {"tile": t - 1}), (has_down, {"tile": t + 1}), (has_prev, {"slab": s - 1}), (has_next, {"slab": s + 1}))

    def remote(src, dst, send, recv, who):
        return pltpu.make_async_remote_copy(
            src_ref=src, dst_ref=dst, send_sem=send, recv_sem=recv, device_id=who, device_id_type=MESH)

    barrier = pltpu.get_barrier_semaphore()
    for there, who in sides:
        @pl.when(there)
        def _():
            pl.semaphore_signal(barrier, inc=1, device_id=who, device_id_type=MESH)
    pl.semaphore_wait(barrier, sum(there.astype(jnp.int32) for there, _ in sides))

    to_up = remote(coarse.at[:, 0], cbuf.at[pl.ds(frames, frames), 3], near_send.at[0], near_recv.at[0], {"tile": t - 1})
    to_down = remote(coarse.at[:, 1], cbuf.at[pl.ds(frames, frames), 0], near_send.at[1], near_recv.at[1], {"tile": t + 1})
    far = [remote(coarse.at[f], cbuf.at[f, pl.ds(1, 2)], far_send.at[f], far_recv.at[f], {"slab": s + 1}) for f in range(frames)]
    hop_up = [remote(cbuf.at[f, 1], cbuf.at[f, 3], hop_send.at[f, 0], hop_recv.at[f, 0], {"tile": t - 1}) for f in range(frames)]
    hop_down = [remote(cbuf.at[f, 2], cbuf.at[f, 0], hop_send.at[f, 1], hop_recv.at[f, 1], {"tile": t + 1}) for f in range(frames)]

    pl.when(has_up)(to_up.start)
    pl.when(has_down)(to_down.start)
    for f in reversed(range(frames)):
        pl.when(has_next)(far[f].start)

    for f in range(frames):
        cbuf[frames + f, 1] = coarse[f, 0]
        cbuf[frames + f, 2] = coarse[f, 1]

    rim = jnp.zeros(cbuf.shape[2:], BF16)

    @pl.when(jnp.logical_not(has_up))
    def _():
        for f in range(frames):
            cbuf[frames + f, 0] = rim

    @pl.when(jnp.logical_not(has_down))
    def _():
        for f in range(frames):
            cbuf[frames + f, 3] = rim

    @pl.when(jnp.logical_or(jnp.logical_not(has_prev), jnp.logical_not(has_up)))
    def _():
        for f in range(frames):
            cbuf[f, 0] = rim

    @pl.when(jnp.logical_or(jnp.logical_not(has_prev), jnp.logical_not(has_down)))
    def _():
        for f in range(frames):
            cbuf[f, 3] = rim

    @pl.when(jnp.logical_not(has_prev))
    def _():
        for f in range(frames):
            cbuf[f, 1] = rim
            cbuf[f, 2] = rim

    half = cols // 2
    lane = lax.broadcasted_iota(jnp.int32, (cols, cols), 0)
    col = lax.broadcasted_iota(jnp.int32, (cols, cols), 1)
    pieces = []
    for j in range(2):
        for b in range(3):
            at = col + (b - 1)
            inside = jnp.logical_and(at >= 0, at < cols)
            hit = jnp.logical_and(inside, lane == j * half + lax.shift_right_arithmetic(at, 1))
            pieces.append(jnp.where(hit, 1.0, 0.0).astype(BF16))
    spread = jnp.concatenate(pieces, axis=1)

    row_col = lax.broadcasted_iota(jnp.int32, (chans, cols), 1)
    first_col = row_col == 0
    last_col = row_col == cols - 1

    def norm_act(values, gain):
        meansq = jnp.mean(values * values, axis=0, keepdims=True)
        y = values * lax.rsqrt(meansq + 1e-06) * gain
        return y / (1.0 + jnp.exp(-y))

    def put(ref, f, r, act):
        ref[f, r, pl.ds(0, chans)] = jnp.where(first_col, 0.0, pltpu.roll(act, 1, 1)).astype(BF16)
        ref[f, r, pl.ds(chans, chans)] = act.astype(BF16)
        ref[f, r, pl.ds(2 * chans, chans)] = jnp.where(last_col, 0.0, pltpu.roll(act, cols - 1, 1)).astype(BF16)

    top_keep = jnp.where(has_up, 1.0, 0.0)
    bottom_keep = jnp.where(has_down, 1.0, 0.0)
    past_keep = jnp.where(has_prev, 1.0, 0.0)

    def row_keep(r, low, high):
        return jnp.where(r < low, top_keep, jnp.where(r >= high, bottom_keep, 1.0))

    def upsample(f):
        def expand(pair, _):
            wide = jnp.dot(cbuf[f, pair], spread, preferred_element_type=F32).astype(BF16)
            stacks = []
            for j in range(2):
                stacks.append(jnp.concatenate([wide[:, (3 * j + b) * cols:(3 * j + b + 1) * cols] for b in range(3)], axis=0))
            got = jnp.dot(wu[...], jnp.concatenate(stacks, axis=1), preferred_element_type=F32)
            part[2 * pair] = got[:, :cols]
            part[2 * pair + 1] = got[:, cols:]
            return _
        lax.fori_loop(0, 4, expand, 0)

        def finish(i, _):
            even = part[i, pl.ds(chans, chans)] + part[i - 1, pl.ds(3 * chans, chans)]
            odd = part[i, pl.ds(2 * chans, chans)] + part[i + 1, pl.ds(0, chans)]
            for j, total in enumerate((even, odd)):
                r = 2 * (i - 1) + j
                value = (total + vecs[0]).astype(BF16)
                if f >= frames:
                    ups[f - frames, r] = value
                act = norm_act(value.astype(F32), vecs[1])
                keep = row_keep(r, 2, rows + 2)
                if f < frames:
                    keep = keep * past_keep
                put(x1, f, r, act * keep)
            return _
        lax.fori_loop(1, 7, finish, 0)

    def conv(x, w, acc, f, last, pairs):
        taps = [tap for tap in range(3) if 0 <= f - tap <= last]
        lo, hi = taps[0], taps[-1] + 1

        def step(p, _):
            r = 2 * p
            lines = [x[f, r + a] for a in range(4)]
            rhs = jnp.concatenate([jnp.concatenate([lines[a], lines[a + 1]], axis=1) for a in range(3)], axis=0)
            got = jnp.dot(w[pl.ds(lo * chans, (hi - lo) * chans)], rhs, preferred_element_type=F32)
            for tap in taps:
                mine = got[(tap - lo) * chans:(tap - lo + 1) * chans]
                acc[f - tap, r] = acc[f - tap, r] + mine[:, :cols]
                acc[f - tap, r + 1] = acc[f - tap, r + 1] + mine[:, cols:]
            return _
        lax.fori_loop(0, pairs, step, 0)

    def second(n):
        def step(r, _):
            act = norm_act(acc1[n, r], vecs[3])
            keep = row_keep(r, 1, rows + 1)
            if n < 2:
                keep = keep * past_keep
            put(x2, n, r, act * keep)
            return _
        lax.fori_loop(0, rows + 2, step, 0)

    mids = frames + 2
    for n in range(mids):
        def fill(r, _):
            acc1[n, r] = vecs[2]
            return _
        lax.fori_loop(0, rows + 2, fill, 0)

    pl.when(has_down)(to_up.wait_recv)
    pl.when(has_up)(to_down.wait_recv)

    def relay(f):
        @pl.when(has_prev)
        def _():
            far[f].wait_recv()
            pl.when(has_up)(hop_up[f].start)
            pl.when(has_down)(hop_down[f].start)

    def landed(f):
        @pl.when(has_prev)
        def _():
            pl.when(has_down)(hop_up[f].wait_recv)
            pl.when(has_up)(hop_down[f].wait_recv)

    for f in reversed(range(frames, 2 * frames)):
        upsample(f)
    for f in reversed(range(frames, 2 * frames)):
        relay(f - frames)
        conv(x1, w1, acc1, f, mids - 1, (rows + 2) // 2)
    for f in reversed(range(frames)):
        landed(f)
        upsample(f)
        conv(x1, w1, acc1, f, mids - 1, (rows + 2) // 2)
    for n in range(mids):
        second(n)

    for n in range(frames):
        def begin(r, _):
            acc2[n, r] = ups[n, r + 2].astype(F32) + vecs[4]
            return _
        lax.fori_loop(0, rows, begin, 0)
    for f in reversed(range(mids)):
        conv(x2, w2, acc2, f, frames - 1, rows // 2)
    for n in range(frames):
        def end(r, _):
            out[n, r] = acc2[n, r].astype(BF16)
            return _
        lax.fori_loop(0, rows, end, 0)

    pl.when(has_up)(to_up.wait_send)
    pl.when(has_down)(to_down.wait_send)
    for f in range(frames):
        pl.when(has_next)(far[f].wait_send)
        pl.when(jnp.logical_and(has_prev, has_up))(hop_up[f].wait_send)
        pl.when(jnp.logical_and(has_prev, has_down))(hop_down[f].wait_send)


def shards(slabs, tiles, coarse, up_weight, up_bias, gain_one, conv_one, bias_one, gain_two, conv_two, bias_two):
    deep, frames, lines, half = coarse.shape
    chans = up_weight.shape[2]
    rows, cols = 2 * lines, 2 * half
    packed = coarse.transpose(1, 2, 0, 3).reshape(frames, lines // 2, 2, deep, half)
    packed = packed.transpose(0, 1, 3, 2, 4).reshape(frames, lines // 2, deep, cols)
    up = up_weight.transpose(0, 2, 1, 3).reshape(3, chans, 3 * deep).astype(F32)
    wu = jnp.concatenate([up[2], up[1] + up[2], up[0] + up[1], up[0]], axis=0).astype(BF16)
    w1 = conv_one.transpose(0, 2, 1, 3).reshape(3 * chans, 9 * chans)
    w2 = conv_two.transpose(0, 2, 1, 3).reshape(3 * chans, 9 * chans)
    vecs = jnp.stack([up_bias, gain_one, bias_one, gain_two, bias_two])
    vecs = jnp.broadcast_to(vecs[:, :, None], (5, chans, cols))
    vmem = pl.BlockSpec(memory_space=pltpu.VMEM)
    got = pl.pallas_call(
        functools.partial(body, slabs, tiles),
        out_shape=jax.ShapeDtypeStruct((frames, rows, chans, cols), BF16),
        in_specs=[vmem] * 5,
        out_specs=vmem,
        scratch_shapes=[
            pltpu.VMEM((2 * frames, 4, deep, cols), BF16),
            pltpu.VMEM((8, 4 * chans, cols), F32),
            pltpu.VMEM((frames, rows + 4, chans, cols), BF16),
            pltpu.VMEM((2 * frames, rows + 4, 3 * chans, cols), BF16),
            pltpu.VMEM((frames + 2, rows + 2, chans, cols), F32),
            pltpu.VMEM((frames + 2, rows + 2, 3 * chans, cols), BF16),
            pltpu.VMEM((frames, rows, chans, cols), F32),
            pltpu.SemaphoreType.DMA((2,)),
            pltpu.SemaphoreType.DMA((2,)),
            pltpu.SemaphoreType.DMA((frames,)),
            pltpu.SemaphoreType.DMA((frames,)),
            pltpu.SemaphoreType.DMA((frames, 2)),
            pltpu.SemaphoreType.DMA((frames, 2)),
        ],
        compiler_params=pltpu.CompilerParams(collective_id=0, has_side_effects=True, vmem_limit_bytes=48 * 2**20),
    )(packed, wu, w1, w2, vecs)
    return got.transpose(2, 0, 1, 3)


def solution(mesh):
    return jax.shard_map(
        functools.partial(shards, mesh.shape["slab"], mesh.shape["tile"]),
        mesh=mesh,
        in_specs=(P(None, "slab", "tile", None), P(), P(), P(), P(), P(), P(), P(), P()),
        out_specs=P(None, "slab", "tile", None),
        check_vma=False,
    )
```

```python
import functools

import jax
import jax.numpy as jnp
from jax import lax
from jax.experimental import pallas as pl
from jax.experimental.pallas import tpu as pltpu
from jax.sharding import PartitionSpec as P

MESH = pl.DeviceIdType.MESH
F32 = jnp.float32
BF16 = jnp.bfloat16


def body(slabs, tiles, coarse, up_w, one_w, two_w, up_b, one_g, one_b, two_g, two_b, out,
         cbuf, wu, w1, w2, vecs, spread, part, ups, x1, acc1, x2, acc2, near_send, near_recv, far_send, far_recv, hop_send, hop_recv):
    frames, _, _, cols = coarse.shape
    chans = out.shape[2]
    rows = out.shape[1]
    s = lax.axis_index("slab")
    t = lax.axis_index("tile")
    has_up, has_down = t > 0, t < tiles - 1
    has_prev, has_next = s > 0, s < slabs - 1
    sides = ((has_up, {"tile": t - 1}), (has_down, {"tile": t + 1}), (has_prev, {"slab": s - 1}), (has_next, {"slab": s + 1}))

    def remote(src, dst, send, recv, who):
        return pltpu.make_async_remote_copy(
            src_ref=src, dst_ref=dst, send_sem=send, recv_sem=recv, device_id=who, device_id_type=MESH)

    barrier = pltpu.get_barrier_semaphore()
    for there, who in sides:
        @pl.when(there)
        def _():
            pl.semaphore_signal(barrier, inc=1, device_id=who, device_id_type=MESH)
    pl.semaphore_wait(barrier, sum(there.astype(jnp.int32) for there, _ in sides))

    to_up = remote(coarse.at[:, 0], cbuf.at[pl.ds(frames, frames), 3], near_send.at[0], near_recv.at[0], {"tile": t - 1})
    to_down = remote(coarse.at[:, 1], cbuf.at[pl.ds(frames, frames), 0], near_send.at[1], near_recv.at[1], {"tile": t + 1})
    far = [remote(coarse.at[f], cbuf.at[f, pl.ds(1, 2)], far_send.at[f], far_recv.at[f], {"slab": s + 1}) for f in range(frames)]
    hop_up = [remote(cbuf.at[f, 1], cbuf.at[f, 3], hop_send.at[f, 0], hop_recv.at[f, 0], {"tile": t - 1}) for f in range(frames)]
    hop_down = [remote(cbuf.at[f, 2], cbuf.at[f, 0], hop_send.at[f, 1], hop_recv.at[f, 1], {"tile": t + 1}) for f in range(frames)]

    pl.when(has_up)(to_up.start)
    pl.when(has_down)(to_down.start)
    for f in reversed(range(frames)):
        pl.when(has_next)(far[f].start)

    for f in range(frames):
        cbuf[frames + f, 1] = coarse[f, 0]
        cbuf[frames + f, 2] = coarse[f, 1]

    rim = jnp.zeros(cbuf.shape[2:], BF16)

    @pl.when(jnp.logical_not(has_up))
    def _():
        for f in range(frames):
            cbuf[frames + f, 0] = rim

    @pl.when(jnp.logical_not(has_down))
    def _():
        for f in range(frames):
            cbuf[frames + f, 3] = rim

    @pl.when(jnp.logical_or(jnp.logical_not(has_prev), jnp.logical_not(has_up)))
    def _():
        for f in range(frames):
            cbuf[f, 0] = rim

    @pl.when(jnp.logical_or(jnp.logical_not(has_prev), jnp.logical_not(has_down)))
    def _():
        for f in range(frames):
            cbuf[f, 3] = rim

    @pl.when(jnp.logical_not(has_prev))
    def _():
        for f in range(frames):
            cbuf[f, 1] = rim
            cbuf[f, 2] = rim

    half = cols // 2
    lane = lax.broadcasted_iota(jnp.int32, (cols, cols), 0)
    col = lax.broadcasted_iota(jnp.int32, (cols, cols), 1)
    for j in range(2):
        hit = lane == j * half + lax.shift_right_arithmetic(col, 1)
        spread[:, j * cols:(j + 1) * cols] = jnp.where(hit, 1.0, 0.0).astype(BF16)

    for n, vec in enumerate((up_b, one_g, one_b, two_g, two_b)):
        vecs[n] = jnp.transpose(jnp.broadcast_to(vec[...], (cols, chans)))
    up = [jnp.concatenate([up_w[a, b] for b in range(3)], axis=1).astype(F32) for a in range(3)]
    for q, mix in enumerate((up[2], up[1] + up[2], up[0] + up[1], up[0])):
        wu[q * chans:(q + 1) * chans] = mix.astype(BF16)
    for raw, w in ((one_w, w1), (two_w, w2)):
        for tap in range(3):
            w[tap * chans:(tap + 1) * chans] = jnp.concatenate([raw[tap, a] for a in range(3)], axis=1)

    row_col = lax.broadcasted_iota(jnp.int32, (1, cols), 1)

    def norm_act(values, gain):
        meansq = jnp.mean(values * values, axis=0, keepdims=True)
        y = values * lax.rsqrt(meansq + 1e-06) * gain
        return y / (1.0 + jnp.exp(-y))

    def shifts(v):
        left = jnp.where(row_col == 0, 0.0, pltpu.roll(v, 1, 1)).astype(BF16)
        right = jnp.where(row_col == cols - 1, 0.0, pltpu.roll(v, cols - 1, 1)).astype(BF16)
        return left, v.astype(BF16), right

    def put(ref, f, r, act):
        pieces = shifts(act)

        def store():
            for b in range(3):
                ref[f, r, pl.ds(b * chans, chans)] = pieces[b]
        return store

    def run(trips, *steps, start=0):
        def trip(i, _):
            for store in [store for step in steps for store in step(i)]:
                store()
            return _
        lax.fori_loop(start, trips, trip, 0)

    top_keep = jnp.where(has_up, 1.0, 0.0)
    bottom_keep = jnp.where(has_down, 1.0, 0.0)
    past_keep = jnp.where(has_prev, 1.0, 0.0)

    def row_keep(r, low, high):
        return jnp.where(r < low, top_keep, jnp.where(r >= high, bottom_keep, 1.0))

    def expand(f):
        slot = f % 2

        def step(pair):
            wide = jnp.dot(cbuf[f, pair], spread[...], preferred_element_type=F32)
            near = [jnp.concatenate(shifts(wide[:, j * cols:(j + 1) * cols]), axis=0) for j in range(2)]
            got = jnp.dot(wu[...], jnp.concatenate(near, axis=1), preferred_element_type=F32)

            def store():
                part[slot, 2 * pair] = got[:, :cols]
                part[slot, 2 * pair + 1] = got[:, cols:]
            return [store]
        return step

    def finish(f, i):
        slot = f % 2
        even = part[slot, i, pl.ds(chans, chans)] + part[slot, i - 1, pl.ds(3 * chans, chans)]
        odd = part[slot, i, pl.ds(2 * chans, chans)] + part[slot, i + 1, pl.ds(0, chans)]
        stores = []
        for j, total in enumerate((even, odd)):
            r = 2 * (i - 1) + j
            value = (total + vecs[0]).astype(BF16)
            act = norm_act(value.astype(F32), vecs[1])
            keep = row_keep(r, 2, rows + 2)
            if f < frames:
                keep = keep * past_keep
            stores.append(put(x1, f, r, act * keep))
            if f >= frames:
                def keep_value(r=r, value=value):
                    ups[f - frames, r] = value
                stores.append(keep_value)
        return stores

    def finish_two(f):
        return lambda i: finish(f, i + 1) + finish(f, jnp.minimum(i + 5, 6))

    def conv(x, w, acc, f, last, start_of, done):
        taps = [tap for tap in range(3) if 0 <= f - tap <= last]
        lo, hi = taps[0], taps[-1] + 1

        def step(p):
            r = 2 * p
            lines = [x[f, r + a] for a in range(4)]
            rhs = jnp.concatenate([jnp.concatenate([lines[a], lines[a + 1]], axis=1) for a in range(3)], axis=0)
            got = jnp.dot(w[pl.ds(lo * chans, (hi - lo) * chans)], rhs, preferred_element_type=F32)

            def store():
                for tap in taps:
                    n = f - tap
                    for j in range(2):
                        mine = got[(tap - lo) * chans:(tap - lo + 1) * chans, j * cols:(j + 1) * cols]
                        total = mine + (start_of(n, r + j) if tap == 2 else acc[n, r + j])
                        if tap == 0 and done is not None:
                            done(n, r + j, total)
                        else:
                            acc[n, r + j] = total
            return [store]
        return step

    mids = frames + 2

    def conv_a(f):
        return conv(x1, w1, acc1, f, mids - 1, lambda n, r: vecs[2], None)

    def finished(n, r, total):
        out[n, r] = total.astype(BF16)

    def conv_b(f):
        return conv(x2, w2, acc2, f, frames - 1, lambda n, r: ups[n, r + 2].astype(F32) + vecs[4], finished)

    def second(n, r):
        act = norm_act(acc1[n, r], vecs[3])
        keep = row_keep(r, 1, rows + 1)
        if n < 2:
            keep = keep * past_keep
        return [put(x2, n, r, act * keep)]

    def second_two(n):
        return lambda p: second(n, 2 * p) + second(n, 2 * p + 1)

    newest = 2 * frames - 1
    run(3, expand(newest), start=1)
    pl.when(has_down)(to_up.wait_recv)
    pl.when(has_up)(to_down.wait_recv)

    def relay(f):
        @pl.when(has_prev)
        def _():
            far[f].wait_recv()
            pl.when(has_up)(hop_up[f].start)
            pl.when(has_down)(hop_down[f].start)

    def landed(f):
        @pl.when(has_prev)
        def _():
            pl.when(has_down)(hop_up[f].wait_recv)
            pl.when(has_up)(hop_down[f].wait_recv)

    run(1, expand(newest))
    run(4, expand(newest), start=3)
    wide_pairs = (rows + 2) // 2
    for f in reversed(range(2 * frames)):
        if 0 < f <= frames:
            landed(f - 1)
        if f > 0:
            run(4, finish_two(f), expand(f - 1))
        else:
            run(4, finish_two(f))
        if f >= frames:
            relay(f - frames)
        ready = f + 1
        if ready < mids:
            run(wide_pairs, second_two(ready), conv_a(f))
        else:
            run(wide_pairs, conv_a(f))
    run(wide_pairs, second_two(0))
    for f in reversed(range(mids)):
        run(rows // 2, conv_b(f))

    pl.when(has_up)(to_up.wait_send)
    pl.when(has_down)(to_down.wait_send)
    for f in range(frames):
        pl.when(has_next)(far[f].wait_send)
        pl.when(jnp.logical_and(has_prev, has_up))(hop_up[f].wait_send)
        pl.when(jnp.logical_and(has_prev, has_down))(hop_down[f].wait_send)


def shards(slabs, tiles, coarse, up_weight, up_bias, gain_one, conv_one, bias_one, gain_two, conv_two, bias_two):
    deep, frames, lines, half = coarse.shape
    chans = up_weight.shape[2]
    rows, cols = 2 * lines, 2 * half
    packed = coarse.transpose(1, 2, 0, 3).reshape(frames, lines // 2, 2, deep, half)
    packed = packed.transpose(0, 1, 3, 2, 4).reshape(frames, lines // 2, deep, cols)
    row = lambda vec: vec.reshape(1, chans)
    vmem = pl.BlockSpec(memory_space=pltpu.VMEM)
    got = pl.pallas_call(
        functools.partial(body, slabs, tiles),
        out_shape=jax.ShapeDtypeStruct((frames, rows, chans, cols), BF16),
        in_specs=[vmem] * 9,
        out_specs=vmem,
        scratch_shapes=[
            pltpu.VMEM((2 * frames, 4, deep, cols), BF16),
            pltpu.VMEM((4 * chans, 3 * deep), BF16),
            pltpu.VMEM((3 * chans, 9 * chans), BF16),
            pltpu.VMEM((3 * chans, 9 * chans), BF16),
            pltpu.VMEM((5, chans, cols), F32),
            pltpu.VMEM((cols, 2 * cols), BF16),
            pltpu.VMEM((2, 8, 4 * chans, cols), F32),
            pltpu.VMEM((frames, rows + 4, chans, cols), BF16),
            pltpu.VMEM((2 * frames, rows + 4, 3 * chans, cols), BF16),
            pltpu.VMEM((frames + 2, rows + 2, chans, cols), F32),
            pltpu.VMEM((frames + 2, rows + 2, 3 * chans, cols), BF16),
            pltpu.VMEM((frames, rows, chans, cols), F32),
            pltpu.SemaphoreType.DMA((2,)),
            pltpu.SemaphoreType.DMA((2,)),
            pltpu.SemaphoreType.DMA((frames,)),
            pltpu.SemaphoreType.DMA((frames,)),
            pltpu.SemaphoreType.DMA((frames, 2)),
            pltpu.SemaphoreType.DMA((frames, 2)),
        ],
        compiler_params=pltpu.CompilerParams(collective_id=0, has_side_effects=True, vmem_limit_bytes=48 * 2**20),
    )(packed, up_weight, conv_one, conv_two, row(up_bias), row(gain_one), row(bias_one), row(gain_two), row(bias_two))
    return got.transpose(2, 0, 1, 3)


def solution(mesh):
    return jax.shard_map(
        functools.partial(shards, mesh.shape["slab"], mesh.shape["tile"]),
        mesh=mesh,
        in_specs=(P(None, "slab", "tile", None), P(), P(), P(), P(), P(), P(), P(), P()),
        out_specs=P(None, "slab", "tile", None),
        check_vma=False,
    )
```

```python
import functools

import jax
import jax.numpy as jnp
from jax import lax
from jax.experimental import pallas as pl
from jax.experimental.pallas import tpu as pltpu
from jax.sharding import PartitionSpec as P

MESH = pl.DeviceIdType.MESH
F32 = jnp.float32
BF16 = jnp.bfloat16


def body(slabs, tiles, coarse, up_w, one_w, two_w, up_b, one_g, one_b, two_g, two_b, out,
         cbuf, wu, w1, w2, vecs, spread, part, ups, x1, acc1, x2, acc2, near_send, near_recv, far_send, far_recv, hop_send, hop_recv):
    frames, _, _, cols = coarse.shape
    chans = out.shape[2]
    rows = out.shape[1]
    s = lax.axis_index("slab")
    t = lax.axis_index("tile")
    has_up, has_down = t > 0, t < tiles - 1
    has_prev, has_next = s > 0, s < slabs - 1
    sides = ((has_up, {"tile": t - 1}), (has_down, {"tile": t + 1}), (has_prev, {"slab": s - 1}), (has_next, {"slab": s + 1}))

    def remote(src, dst, send, recv, who):
        return pltpu.make_async_remote_copy(
            src_ref=src, dst_ref=dst, send_sem=send, recv_sem=recv, device_id=who, device_id_type=MESH)

    barrier = pltpu.get_barrier_semaphore()
    for there, who in sides:
        @pl.when(there)
        def _():
            pl.semaphore_signal(barrier, inc=1, device_id=who, device_id_type=MESH)
    pl.semaphore_wait(barrier, sum(there.astype(jnp.int32) for there, _ in sides))

    to_up = remote(coarse.at[:, 0], cbuf.at[pl.ds(frames, frames), 3], near_send.at[0], near_recv.at[0], {"tile": t - 1})
    to_down = remote(coarse.at[:, 1], cbuf.at[pl.ds(frames, frames), 0], near_send.at[1], near_recv.at[1], {"tile": t + 1})
    far = [remote(coarse.at[f], cbuf.at[f, pl.ds(1, 2)], far_send.at[f], far_recv.at[f], {"slab": s + 1}) for f in range(frames)]
    hop_up = [remote(cbuf.at[f, 1], cbuf.at[f, 3], hop_send.at[f, 0], hop_recv.at[f, 0], {"tile": t - 1}) for f in range(frames)]
    hop_down = [remote(cbuf.at[f, 2], cbuf.at[f, 0], hop_send.at[f, 1], hop_recv.at[f, 1], {"tile": t + 1}) for f in range(frames)]

    pl.when(has_up)(to_up.start)
    pl.when(has_down)(to_down.start)
    for f in reversed(range(frames)):
        pl.when(has_next)(far[f].start)

    for f in range(frames):
        cbuf[frames + f, 1] = coarse[f, 0]
        cbuf[frames + f, 2] = coarse[f, 1]

    rim = jnp.zeros(cbuf.shape[2:], BF16)

    @pl.when(jnp.logical_not(has_up))
    def _():
        for f in range(frames):
            cbuf[frames + f, 0] = rim

    @pl.when(jnp.logical_not(has_down))
    def _():
        for f in range(frames):
            cbuf[frames + f, 3] = rim

    @pl.when(jnp.logical_or(jnp.logical_not(has_prev), jnp.logical_not(has_up)))
    def _():
        for f in range(frames):
            cbuf[f, 0] = rim

    @pl.when(jnp.logical_or(jnp.logical_not(has_prev), jnp.logical_not(has_down)))
    def _():
        for f in range(frames):
            cbuf[f, 3] = rim

    @pl.when(jnp.logical_not(has_prev))
    def _():
        for f in range(frames):
            cbuf[f, 1] = rim
            cbuf[f, 2] = rim

    half = cols // 2
    lane = lax.broadcasted_iota(jnp.int32, (cols, cols), 0)
    col = lax.broadcasted_iota(jnp.int32, (cols, cols), 1)
    for j in range(2):
        hit = lane == j * half + lax.shift_right_arithmetic(col, 1)
        spread[:, j * cols:(j + 1) * cols] = jnp.where(hit, 1.0, 0.0).astype(BF16)

    for n, vec in enumerate((up_b, one_g, one_b, two_g, two_b)):
        vecs[n] = jnp.transpose(jnp.broadcast_to(vec[...], (cols, chans)))
    up = [jnp.concatenate([up_w[a, b] for b in range(3)], axis=1).astype(F32) for a in range(3)]
    for q, mix in enumerate((up[2], up[1] + up[2], up[0] + up[1], up[0])):
        wu[q * chans:(q + 1) * chans] = mix.astype(BF16)
    for raw, w in ((one_w, w1), (two_w, w2)):
        for tap in range(3):
            w[tap * chans:(tap + 1) * chans] = jnp.concatenate([raw[tap, a] for a in range(3)], axis=1)

    row_col = lax.broadcasted_iota(jnp.int32, (1, cols), 1)

    def norm_act(values, gain):
        meansq = jnp.mean(values * values, axis=0, keepdims=True)
        y = values * lax.rsqrt(meansq + 1e-06) * gain
        return y / (1.0 + jnp.exp(-y))

    def shifts(v):
        left = jnp.where(row_col == 0, 0.0, pltpu.roll(v, 1, 1)).astype(BF16)
        right = jnp.where(row_col == cols - 1, 0.0, pltpu.roll(v, cols - 1, 1)).astype(BF16)
        return left, v.astype(BF16), right

    def put(ref, f, r, act):
        pieces = shifts(act)

        def store():
            for b in range(3):
                ref[f, r, pl.ds(b * chans, chans)] = pieces[b]
        return store

    def run(trips, *steps):
        def trip(i, _):
            for store in [store for step in steps for store in step(i)]:
                store()
            return _
        lax.fori_loop(0, trips, trip, 0)

    top_keep = jnp.where(has_up, 1.0, 0.0)
    bottom_keep = jnp.where(has_down, 1.0, 0.0)
    past_keep = jnp.where(has_prev, 1.0, 0.0)

    def row_keep(r, low, high):
        if isinstance(r, int):
            return top_keep if r < low else bottom_keep if r >= high else 1.0
        return jnp.where(r < low, top_keep, jnp.where(r >= high, bottom_keep, 1.0))

    def expand(f):
        slot = f % 2

        def step(pair):
            wide = jnp.dot(cbuf[f, pair], spread[...], preferred_element_type=F32)
            near = [jnp.concatenate(shifts(wide[:, j * cols:(j + 1) * cols]), axis=0) for j in range(2)]
            lo = chans if pair == 0 else 0
            hi = 3 * chans if pair == 3 else 4 * chans
            got = jnp.dot(wu[lo:hi], jnp.concatenate(near, axis=1), preferred_element_type=F32)

            def store():
                part[slot, 2 * pair, lo:hi] = got[:, :cols]
                part[slot, 2 * pair + 1, lo:hi] = got[:, cols:]
            return [store]
        return step

    def finish(f, i):
        slot = f % 2
        even = part[slot, i, pl.ds(chans, chans)] + part[slot, i - 1, pl.ds(3 * chans, chans)]
        odd = part[slot, i, pl.ds(2 * chans, chans)] + part[slot, i + 1, pl.ds(0, chans)]
        stores = []
        for j, total in enumerate((even, odd)):
            r = 2 * (i - 1) + j
            value = (total + vecs[0]).astype(BF16)
            act = norm_act(value.astype(F32), vecs[1])
            keep = row_keep(r, 2, rows + 2)
            if f < frames:
                keep = keep * past_keep
            stores.append(put(x1, f, r, act * keep))
            if f >= frames:
                def keep_value(r=r, value=value):
                    ups[f - frames, r] = value
                stores.append(keep_value)
        return stores

    turns = ((1,), (2, 3), (4,), (5, 6))

    def level(old, new):
        for k in range(4):
            stores = [store for i in turns[k] for store in finish(old, i)]
            if new is not None:
                stores += expand(new)(k)
            for store in stores:
                store()

    def conv(x, w, acc, f, last, start_of, done):
        taps = [tap for tap in range(3) if 0 <= f - tap <= last]
        lo, hi = taps[0], taps[-1] + 1

        def step(p):
            r = 2 * p
            lines = [x[f, r + a] for a in range(4)]
            rhs = jnp.concatenate([jnp.concatenate([lines[a], lines[a + 1]], axis=1) for a in range(3)], axis=0)
            got = jnp.dot(w[pl.ds(lo * chans, (hi - lo) * chans)], rhs, preferred_element_type=F32)

            def store():
                for tap in taps:
                    n = f - tap
                    for j in range(2):
                        mine = got[(tap - lo) * chans:(tap - lo + 1) * chans, j * cols:(j + 1) * cols]
                        total = mine + (start_of(n, r + j) if tap == 2 else acc[n, r + j])
                        if tap == 0 and done is not None:
                            done(n, r + j, total)
                        else:
                            acc[n, r + j] = total
            return [store]
        return step

    mids = frames + 2

    def conv_a(f):
        return conv(x1, w1, acc1, f, mids - 1, lambda n, r: vecs[2], None)

    def finished(n, r, total):
        out[n, r] = total.astype(BF16)

    def conv_b(f):
        return conv(x2, w2, acc2, f, frames - 1, lambda n, r: ups[n, r + 2].astype(F32) + vecs[4], finished)

    def second(n, r):
        act = norm_act(acc1[n, r], vecs[3])
        keep = row_keep(r, 1, rows + 1)
        if n < 2:
            keep = keep * past_keep
        return [put(x2, n, r, act * keep)]

    def second_two(n):
        return lambda p: second(n, 2 * p) + second(n, 2 * p + 1)

    newest = 2 * frames - 1
    def lone(pairs):
        for pair in pairs:
            for store in expand(newest)(pair):
                store()

    lone((1, 2))
    pl.when(has_down)(to_up.wait_recv)
    pl.when(has_up)(to_down.wait_recv)

    def relay(f):
        @pl.when(has_prev)
        def _():
            far[f].wait_recv()
            pl.when(has_up)(hop_up[f].start)
            pl.when(has_down)(hop_down[f].start)

    def landed(f):
        @pl.when(has_prev)
        def _():
            pl.when(has_down)(hop_up[f].wait_recv)
            pl.when(has_up)(hop_down[f].wait_recv)

    lone((0, 3))
    wide_pairs = (rows + 2) // 2
    for f in reversed(range(2 * frames)):
        if 0 < f <= frames:
            landed(f - 1)
        level(f, f - 1 if f > 0 else None)
        if f >= frames:
            relay(f - frames)
        ready = f + 1
        if ready < mids:
            run(wide_pairs, second_two(ready), conv_a(f))
        else:
            run(wide_pairs, conv_a(f))
    run(wide_pairs, second_two(0))
    for f in reversed(range(mids)):
        run(rows // 2, conv_b(f))

    pl.when(has_up)(to_up.wait_send)
    pl.when(has_down)(to_down.wait_send)
    for f in range(frames):
        pl.when(has_next)(far[f].wait_send)
        pl.when(jnp.logical_and(has_prev, has_up))(hop_up[f].wait_send)
        pl.when(jnp.logical_and(has_prev, has_down))(hop_down[f].wait_send)


def shards(slabs, tiles, coarse, up_weight, up_bias, gain_one, conv_one, bias_one, gain_two, conv_two, bias_two):
    deep, frames, lines, half = coarse.shape
    chans = up_weight.shape[2]
    rows, cols = 2 * lines, 2 * half
    packed = coarse.transpose(1, 2, 0, 3).reshape(frames, lines // 2, 2, deep, half)
    packed = packed.transpose(0, 1, 3, 2, 4).reshape(frames, lines // 2, deep, cols)
    row = lambda vec: vec.reshape(1, chans)
    vmem = pl.BlockSpec(memory_space=pltpu.VMEM)
    got = pl.pallas_call(
        functools.partial(body, slabs, tiles),
        out_shape=jax.ShapeDtypeStruct((frames, rows, chans, cols), BF16),
        in_specs=[vmem] * 9,
        out_specs=vmem,
        scratch_shapes=[
            pltpu.VMEM((2 * frames, 4, deep, cols), BF16),
            pltpu.VMEM((4 * chans, 3 * deep), BF16),
            pltpu.VMEM((3 * chans, 9 * chans), BF16),
            pltpu.VMEM((3 * chans, 9 * chans), BF16),
            pltpu.VMEM((5, chans, cols), F32),
            pltpu.VMEM((cols, 2 * cols), BF16),
            pltpu.VMEM((2, 8, 4 * chans, cols), F32),
            pltpu.VMEM((frames, rows + 4, chans, cols), BF16),
            pltpu.VMEM((2 * frames, rows + 4, 3 * chans, cols), BF16),
            pltpu.VMEM((frames + 2, rows + 2, chans, cols), F32),
            pltpu.VMEM((frames + 2, rows + 2, 3 * chans, cols), BF16),
            pltpu.VMEM((frames, rows, chans, cols), F32),
            pltpu.SemaphoreType.DMA((2,)),
            pltpu.SemaphoreType.DMA((2,)),
            pltpu.SemaphoreType.DMA((frames,)),
            pltpu.SemaphoreType.DMA((frames,)),
            pltpu.SemaphoreType.DMA((frames, 2)),
            pltpu.SemaphoreType.DMA((frames, 2)),
        ],
        compiler_params=pltpu.CompilerParams(collective_id=0, has_side_effects=True, vmem_limit_bytes=48 * 2**20),
    )(packed, up_weight, conv_one, conv_two, row(up_bias), row(gain_one), row(bias_one), row(gain_two), row(bias_two))
    return got.transpose(2, 0, 1, 3)


def solution(mesh):
    return jax.shard_map(
        functools.partial(shards, mesh.shape["slab"], mesh.shape["tile"]),
        mesh=mesh,
        in_specs=(P(None, "slab", "tile", None), P(), P(), P(), P(), P(), P(), P(), P()),
        out_specs=P(None, "slab", "tile", None),
        check_vma=False,
    )
```

```python
import functools

import jax
import jax.numpy as jnp
from jax import lax
from jax.experimental import pallas as pl
from jax.experimental.pallas import tpu as pltpu
from jax.sharding import PartitionSpec as P

MESH = pl.DeviceIdType.MESH
F32 = jnp.float32
BF16 = jnp.bfloat16


def body(slabs, tiles, coarse, up_hbm, one_hbm, two_hbm, up_b, one_g, one_b, two_g, two_b, out,
         up_w, one_w, two_w, load, cbuf, wu, w1, w2, vecs, spread, part, ups, x1, acc1, x2, acc2, near_send, near_recv, far_send, far_recv, hop_send, hop_recv):
    frames, _, _, cols = coarse.shape
    chans = out.shape[2]
    rows = out.shape[1]
    s = lax.axis_index("slab")
    t = lax.axis_index("tile")
    has_up, has_down = t > 0, t < tiles - 1
    has_prev, has_next = s > 0, s < slabs - 1
    sides = ((has_up, {"tile": t - 1}), (has_down, {"tile": t + 1}), (has_prev, {"slab": s - 1}), (has_next, {"slab": s + 1}))

    def remote(src, dst, send, recv, who):
        return pltpu.make_async_remote_copy(
            src_ref=src, dst_ref=dst, send_sem=send, recv_sem=recv, device_id=who, device_id_type=MESH)

    loads = [pltpu.make_async_copy(src, dst, load.at[n])
             for n, (src, dst) in enumerate(((up_hbm, up_w), (one_hbm, one_w), (two_hbm, two_w)))]
    for copy in loads:
        copy.start()

    barrier = pltpu.get_barrier_semaphore()
    for there, who in sides:
        @pl.when(there)
        def _():
            pl.semaphore_signal(barrier, inc=1, device_id=who, device_id_type=MESH)
    pl.semaphore_wait(barrier, sum(there.astype(jnp.int32) for there, _ in sides))

    to_up = remote(coarse.at[:, 0], cbuf.at[pl.ds(frames, frames), 3], near_send.at[0], near_recv.at[0], {"tile": t - 1})
    to_down = remote(coarse.at[:, 1], cbuf.at[pl.ds(frames, frames), 0], near_send.at[1], near_recv.at[1], {"tile": t + 1})
    far = [remote(coarse.at[f], cbuf.at[f, pl.ds(1, 2)], far_send.at[f], far_recv.at[f], {"slab": s + 1}) for f in range(frames)]
    hop_up = [remote(cbuf.at[f, 1], cbuf.at[f, 3], hop_send.at[f, 0], hop_recv.at[f, 0], {"tile": t - 1}) for f in range(frames)]
    hop_down = [remote(cbuf.at[f, 2], cbuf.at[f, 0], hop_send.at[f, 1], hop_recv.at[f, 1], {"tile": t + 1}) for f in range(frames)]

    pl.when(has_up)(to_up.start)
    pl.when(has_down)(to_down.start)
    for f in reversed(range(frames)):
        pl.when(has_next)(far[f].start)

    for f in range(frames):
        cbuf[frames + f, 1] = coarse[f, 0]
        cbuf[frames + f, 2] = coarse[f, 1]

    rim = jnp.zeros(cbuf.shape[2:], BF16)

    @pl.when(jnp.logical_not(has_up))
    def _():
        for f in range(frames):
            cbuf[frames + f, 0] = rim

    @pl.when(jnp.logical_not(has_down))
    def _():
        for f in range(frames):
            cbuf[frames + f, 3] = rim

    @pl.when(jnp.logical_or(jnp.logical_not(has_prev), jnp.logical_not(has_up)))
    def _():
        for f in range(frames):
            cbuf[f, 0] = rim

    @pl.when(jnp.logical_or(jnp.logical_not(has_prev), jnp.logical_not(has_down)))
    def _():
        for f in range(frames):
            cbuf[f, 3] = rim

    @pl.when(jnp.logical_not(has_prev))
    def _():
        for f in range(frames):
            cbuf[f, 1] = rim
            cbuf[f, 2] = rim

    half = cols // 2
    lane = lax.broadcasted_iota(jnp.int32, (cols, cols), 0)
    col = lax.broadcasted_iota(jnp.int32, (cols, cols), 1)
    for j in range(2):
        hit = lane == j * half + lax.shift_right_arithmetic(col, 1)
        spread[:, j * cols:(j + 1) * cols] = jnp.where(hit, 1.0, 0.0).astype(BF16)

    for n, vec in enumerate((up_b, one_g, one_b, two_g, two_b)):
        vecs[n] = jnp.transpose(jnp.broadcast_to(vec[...], (cols, chans)))
    loads[0].wait()
    up = [jnp.concatenate([up_w[a, b] for b in range(3)], axis=1).astype(F32) for a in range(3)]
    for q, mix in enumerate((up[2], up[1] + up[2], up[0] + up[1], up[0])):
        wu[q * chans:(q + 1) * chans] = mix.astype(BF16)
    row_col = lax.broadcasted_iota(jnp.int32, (1, cols), 1)

    def norm_act(values, gain):
        meansq = jnp.mean(values * values, axis=0, keepdims=True)
        y = values * lax.rsqrt(meansq + 1e-06) * gain
        return y / (1.0 + jnp.exp(-y))

    def shifts(v):
        left = jnp.where(row_col == 0, 0.0, pltpu.roll(v, 1, 1)).astype(BF16)
        right = jnp.where(row_col == cols - 1, 0.0, pltpu.roll(v, cols - 1, 1)).astype(BF16)
        return left, v.astype(BF16), right

    def put(ref, f, r, act):
        pieces = shifts(act)

        def store():
            for b in range(3):
                ref[f, r, pl.ds(b * chans, chans)] = pieces[b]
        return store

    def run(trips, *steps):
        def trip(i, _):
            for store in [store for step in steps for store in step(i)]:
                store()
            return _
        lax.fori_loop(0, trips, trip, 0)

    top_keep = jnp.where(has_up, 1.0, 0.0)
    bottom_keep = jnp.where(has_down, 1.0, 0.0)
    past_keep = jnp.where(has_prev, 1.0, 0.0)

    def row_keep(r, low, high):
        if isinstance(r, int):
            return top_keep if r < low else bottom_keep if r >= high else 1.0
        return jnp.where(r < low, top_keep, jnp.where(r >= high, bottom_keep, 1.0))

    def expand(f):
        slot = f % 2

        def step(pair):
            wide = jnp.dot(cbuf[f, pair], spread[...], preferred_element_type=F32)
            near = [jnp.concatenate(shifts(wide[:, j * cols:(j + 1) * cols]), axis=0) for j in range(2)]
            lo = chans if pair == 0 else 0
            hi = 3 * chans if pair == 3 else 4 * chans
            got = jnp.dot(wu[lo:hi], jnp.concatenate(near, axis=1), preferred_element_type=F32)

            def store():
                part[slot, 2 * pair, lo:hi] = got[:, :cols]
                part[slot, 2 * pair + 1, lo:hi] = got[:, cols:]
            return [store]
        return step

    def finish(f, i):
        slot = f % 2
        even = part[slot, i, pl.ds(chans, chans)] + part[slot, i - 1, pl.ds(3 * chans, chans)]
        odd = part[slot, i, pl.ds(2 * chans, chans)] + part[slot, i + 1, pl.ds(0, chans)]
        stores = []
        for j, total in enumerate((even, odd)):
            r = 2 * (i - 1) + j
            value = (total + vecs[0]).astype(BF16)
            act = norm_act(value.astype(F32), vecs[1])
            keep = row_keep(r, 2, rows + 2)
            if f < frames:
                keep = keep * past_keep
            stores.append(put(x1, f, r, act * keep))
            if f >= frames:
                def keep_value(r=r, value=value):
                    ups[f - frames, r] = value
                stores.append(keep_value)
        return stores

    turns = ((1,), (2, 3), (4,), (5, 6))

    def level(old, new):
        for k in range(4):
            stores = [store for i in turns[k] for store in finish(old, i)]
            if new is not None:
                stores += expand(new)(k)
            for store in stores:
                store()

    def conv(x, w, acc, f, last, start_of, done):
        taps = [tap for tap in range(3) if 0 <= f - tap <= last]
        lo, hi = taps[0], taps[-1] + 1

        def step(p):
            r = 2 * p
            lines = [x[f, r + a] for a in range(4)]
            rhs = jnp.concatenate([jnp.concatenate([lines[a], lines[a + 1]], axis=1) for a in range(3)], axis=0)
            got = jnp.dot(w[pl.ds(lo * chans, (hi - lo) * chans)], rhs, preferred_element_type=F32)

            def store():
                for tap in taps:
                    n = f - tap
                    for j in range(2):
                        mine = got[(tap - lo) * chans:(tap - lo + 1) * chans, j * cols:(j + 1) * cols]
                        total = mine + (start_of(n, r + j) if tap == 2 else acc[n, r + j])
                        if tap == 0 and done is not None:
                            done(n, r + j, total)
                        else:
                            acc[n, r + j] = total
            return [store]
        return step

    mids = frames + 2

    def conv_a(f):
        return conv(x1, w1, acc1, f, mids - 1, lambda n, r: vecs[2], None)

    def finished(n, r, total):
        out[n, r] = total.astype(BF16)

    def conv_b(f):
        return conv(x2, w2, acc2, f, frames - 1, lambda n, r: ups[n, r + 2].astype(F32) + vecs[4], finished)

    def second(n, r):
        act = norm_act(acc1[n, r], vecs[3])
        keep = row_keep(r, 1, rows + 1)
        if n < 2:
            keep = keep * past_keep
        return [put(x2, n, r, act * keep)]

    def second_two(n):
        return lambda p: second(n, 2 * p) + second(n, 2 * p + 1)

    newest = 2 * frames - 1
    def lone(pairs):
        for pair in pairs:
            for store in expand(newest)(pair):
                store()

    lone((1, 2))
    for copy, raw, w in ((loads[1], one_w, w1), (loads[2], two_w, w2)):
        copy.wait()
        for tap in range(3):
            w[tap * chans:(tap + 1) * chans] = jnp.concatenate([raw[tap, a] for a in range(3)], axis=1)
    pl.when(has_down)(to_up.wait_recv)
    pl.when(has_up)(to_down.wait_recv)

    def relay(f):
        @pl.when(has_prev)
        def _():
            far[f].wait_recv()
            pl.when(has_up)(hop_up[f].start)
            pl.when(has_down)(hop_down[f].start)

    def landed(f):
        @pl.when(has_prev)
        def _():
            pl.when(has_down)(hop_up[f].wait_recv)
            pl.when(has_up)(hop_down[f].wait_recv)

    lone((0, 3))
    wide_pairs = (rows + 2) // 2
    for f in reversed(range(2 * frames)):
        if 0 < f <= frames:
            landed(f - 1)
        level(f, f - 1 if f > 0 else None)
        if f >= frames:
            relay(f - frames)
        ready = f + 1
        if ready < mids:
            run(wide_pairs, second_two(ready), conv_a(f))
        else:
            run(wide_pairs, conv_a(f))
    run(wide_pairs, second_two(0))
    for f in reversed(range(mids)):
        run(rows // 2, conv_b(f))

    pl.when(has_up)(to_up.wait_send)
    pl.when(has_down)(to_down.wait_send)
    for f in range(frames):
        pl.when(has_next)(far[f].wait_send)
        pl.when(jnp.logical_and(has_prev, has_up))(hop_up[f].wait_send)
        pl.when(jnp.logical_and(has_prev, has_down))(hop_down[f].wait_send)


def shards(slabs, tiles, coarse, up_weight, up_bias, gain_one, conv_one, bias_one, gain_two, conv_two, bias_two):
    deep, frames, lines, half = coarse.shape
    chans = up_weight.shape[2]
    rows, cols = 2 * lines, 2 * half
    packed = coarse.transpose(1, 2, 0, 3).reshape(frames, lines // 2, 2, deep, half)
    packed = packed.transpose(0, 1, 3, 2, 4).reshape(frames, lines // 2, deep, cols)
    row = lambda vec: vec.reshape(1, chans)
    vmem = pl.BlockSpec(memory_space=pltpu.VMEM)
    hbm = pl.BlockSpec(memory_space=pltpu.HBM)
    got = pl.pallas_call(
        functools.partial(body, slabs, tiles),
        out_shape=jax.ShapeDtypeStruct((frames, rows, chans, cols), BF16),
        in_specs=[vmem] + [hbm] * 3 + [vmem] * 5,
        out_specs=vmem,
        scratch_shapes=[
            pltpu.VMEM(up_weight.shape, BF16),
            pltpu.VMEM(conv_one.shape, BF16),
            pltpu.VMEM(conv_two.shape, BF16),
            pltpu.SemaphoreType.DMA((3,)),
            pltpu.VMEM((2 * frames, 4, deep, cols), BF16),
            pltpu.VMEM((4 * chans, 3 * deep), BF16),
            pltpu.VMEM((3 * chans, 9 * chans), BF16),
            pltpu.VMEM((3 * chans, 9 * chans), BF16),
            pltpu.VMEM((5, chans, cols), F32),
            pltpu.VMEM((cols, 2 * cols), BF16),
            pltpu.VMEM((2, 8, 4 * chans, cols), F32),
            pltpu.VMEM((frames, rows + 4, chans, cols), BF16),
            pltpu.VMEM((2 * frames, rows + 4, 3 * chans, cols), BF16),
            pltpu.VMEM((frames + 2, rows + 2, chans, cols), F32),
            pltpu.VMEM((frames + 2, rows + 2, 3 * chans, cols), BF16),
            pltpu.VMEM((frames, rows, chans, cols), F32),
            pltpu.SemaphoreType.DMA((2,)),
            pltpu.SemaphoreType.DMA((2,)),
            pltpu.SemaphoreType.DMA((frames,)),
            pltpu.SemaphoreType.DMA((frames,)),
            pltpu.SemaphoreType.DMA((frames, 2)),
            pltpu.SemaphoreType.DMA((frames, 2)),
        ],
        compiler_params=pltpu.CompilerParams(collective_id=0, has_side_effects=True, vmem_limit_bytes=63950000),
    )(packed, up_weight, conv_one, conv_two, row(up_bias), row(gain_one), row(bias_one), row(gain_two), row(bias_two))
    return got.transpose(2, 0, 1, 3)


def solution(mesh):
    return jax.shard_map(
        functools.partial(shards, mesh.shape["slab"], mesh.shape["tile"]),
        mesh=mesh,
        in_specs=(P(None, "slab", "tile", None), P(), P(), P(), P(), P(), P(), P(), P()),
        out_specs=P(None, "slab", "tile", None),
        check_vma=False,
    )
```

```python
import functools

import jax
import jax.numpy as jnp
from jax import lax
from jax.experimental import pallas as pl
from jax.experimental.pallas import tpu as pltpu
from jax.sharding import PartitionSpec as P

MESH = pl.DeviceIdType.MESH
F32 = jnp.float32
BF16 = jnp.bfloat16


def body(slabs, tiles, coarse, up_w, one_w, two_w, up_b, one_g, one_b, two_g, two_b, out,
         cbuf, wu, w1, w2, vecs, spread, part, ups, x1, acc1, x2, acc2, near_send, near_recv, far_send, far_recv, hop_send, hop_recv):
    frames, _, _, cols = coarse.shape
    chans = out.shape[2]
    rows = out.shape[1]
    s = lax.axis_index("slab")
    t = lax.axis_index("tile")
    has_up, has_down = t > 0, t < tiles - 1
    has_prev, has_next = s > 0, s < slabs - 1
    sides = ((has_up, {"tile": t - 1}), (has_down, {"tile": t + 1}), (has_prev, {"slab": s - 1}), (has_next, {"slab": s + 1}))

    def remote(src, dst, send, recv, who):
        return pltpu.make_async_remote_copy(
            src_ref=src, dst_ref=dst, send_sem=send, recv_sem=recv, device_id=who, device_id_type=MESH)

    barrier = pltpu.get_barrier_semaphore()
    for there, who in sides:
        @pl.when(there)
        def _():
            pl.semaphore_signal(barrier, inc=1, device_id=who, device_id_type=MESH)
    pl.semaphore_wait(barrier, sum(there.astype(jnp.int32) for there, _ in sides))

    to_up = remote(coarse.at[:, 0], cbuf.at[pl.ds(frames, frames), 3], near_send.at[0], near_recv.at[0], {"tile": t - 1})
    to_down = remote(coarse.at[:, 1], cbuf.at[pl.ds(frames, frames), 0], near_send.at[1], near_recv.at[1], {"tile": t + 1})
    far = [remote(coarse.at[f], cbuf.at[f, pl.ds(1, 2)], far_send.at[f], far_recv.at[f], {"slab": s + 1}) for f in range(frames)]
    hop_up = [remote(cbuf.at[f, 1], cbuf.at[f, 3], hop_send.at[f, 0], hop_recv.at[f, 0], {"tile": t - 1}) for f in range(frames)]
    hop_down = [remote(cbuf.at[f, 2], cbuf.at[f, 0], hop_send.at[f, 1], hop_recv.at[f, 1], {"tile": t + 1}) for f in range(frames)]

    pl.when(has_up)(to_up.start)
    pl.when(has_down)(to_down.start)
    for f in reversed(range(frames)):
        pl.when(has_next)(far[f].start)

    for f in range(frames):
        cbuf[frames + f, 1] = coarse[f, 0]
        cbuf[frames + f, 2] = coarse[f, 1]

    rim = jnp.zeros(cbuf.shape[2:], BF16)

    @pl.when(jnp.logical_not(has_up))
    def _():
        for f in range(frames):
            cbuf[frames + f, 0] = rim

    @pl.when(jnp.logical_not(has_down))
    def _():
        for f in range(frames):
            cbuf[frames + f, 3] = rim

    @pl.when(jnp.logical_or(jnp.logical_not(has_prev), jnp.logical_not(has_up)))
    def _():
        for f in range(frames):
            cbuf[f, 0] = rim

    @pl.when(jnp.logical_or(jnp.logical_not(has_prev), jnp.logical_not(has_down)))
    def _():
        for f in range(frames):
            cbuf[f, 3] = rim

    @pl.when(jnp.logical_not(has_prev))
    def _():
        for f in range(frames):
            cbuf[f, 1] = rim
            cbuf[f, 2] = rim

    half = cols // 2
    lane = lax.broadcasted_iota(jnp.int32, (cols, cols), 0)
    col = lax.broadcasted_iota(jnp.int32, (cols, cols), 1)
    for j in range(2):
        hit = lane == j * half + lax.shift_right_arithmetic(col, 1)
        spread[:, j * cols:(j + 1) * cols] = jnp.where(hit, 1.0, 0.0).astype(BF16)

    for n, vec in enumerate((up_b, one_g, one_b, two_g, two_b)):
        vecs[n] = jnp.transpose(jnp.broadcast_to(vec[...], (cols, chans)))
    up = [jnp.concatenate([up_w[a, b] for b in range(3)], axis=1).astype(F32) for a in range(3)]
    for q, mix in enumerate((up[2], up[1] + up[2], up[0] + up[1], up[0])):
        wu[q * chans:(q + 1) * chans] = mix.astype(BF16)
    for raw, w in ((one_w, w1), (two_w, w2)):
        for tap in range(3):
            w[tap * chans:(tap + 1) * chans] = jnp.concatenate([raw[tap, a] for a in range(3)], axis=1)

    row_col = lax.broadcasted_iota(jnp.int32, (1, cols), 1)

    def norm_act(values, gain):
        meansq = jnp.mean(values * values, axis=0, keepdims=True)
        y = values * lax.rsqrt(meansq + 1e-06) * gain
        return y / (1.0 + jnp.exp(-y))

    def shifts(v):
        left = jnp.where(row_col == 0, 0.0, pltpu.roll(v, 1, 1)).astype(BF16)
        right = jnp.where(row_col == cols - 1, 0.0, pltpu.roll(v, cols - 1, 1)).astype(BF16)
        return left, v.astype(BF16), right

    def put(ref, f, r, act):
        pieces = shifts(act)

        def store():
            for b in range(3):
                ref[f, r, pl.ds(b * chans, chans)] = pieces[b]
        return store

    def run(trips, *steps):
        for i in range(trips):
            for store in [store for step in steps for store in step(i)]:
                store()

    top_keep = jnp.where(has_up, 1.0, 0.0)
    bottom_keep = jnp.where(has_down, 1.0, 0.0)
    past_keep = jnp.where(has_prev, 1.0, 0.0)

    def row_keep(r, low, high):
        if isinstance(r, int):
            return top_keep if r < low else bottom_keep if r >= high else 1.0
        return jnp.where(r < low, top_keep, jnp.where(r >= high, bottom_keep, 1.0))

    def expand(f):
        slot = f % 2

        def step(pair):
            wide = jnp.dot(cbuf[f, pair], spread[...], preferred_element_type=F32)
            near = [jnp.concatenate(shifts(wide[:, j * cols:(j + 1) * cols]), axis=0) for j in range(2)]
            lo = chans if pair == 0 else 0
            hi = 3 * chans if pair == 3 else 4 * chans
            got = jnp.dot(wu[lo:hi], jnp.concatenate(near, axis=1), preferred_element_type=F32)

            def store():
                part[slot, 2 * pair, lo:hi] = got[:, :cols]
                part[slot, 2 * pair + 1, lo:hi] = got[:, cols:]
            return [store]
        return step

    def finish(f, i):
        slot = f % 2
        even = part[slot, i, pl.ds(chans, chans)] + part[slot, i - 1, pl.ds(3 * chans, chans)]
        odd = part[slot, i, pl.ds(2 * chans, chans)] + part[slot, i + 1, pl.ds(0, chans)]
        stores = []
        for j, total in enumerate((even, odd)):
            r = 2 * (i - 1) + j
            value = (total + vecs[0]).astype(BF16)
            act = norm_act(value.astype(F32), vecs[1])
            keep = row_keep(r, 2, rows + 2)
            if f < frames:
                keep = keep * past_keep
            stores.append(put(x1, f, r, act * keep))
            if f >= frames:
                def keep_value(r=r, value=value):
                    ups[f - frames, r] = value
                stores.append(keep_value)
        return stores

    turns = ((1,), (2, 3), (4,), (5, 6))

    def level(old, new):
        for k in range(4):
            stores = [store for i in turns[k] for store in finish(old, i)]
            if new is not None:
                stores += expand(new)(k)
            for store in stores:
                store()

    def conv(x, w, acc, f, last, start_of, done):
        taps = [tap for tap in range(3) if 0 <= f - tap <= last]
        lo, hi = taps[0], taps[-1] + 1

        def step(p):
            r = 2 * p
            lines = [x[f, r + a] for a in range(4)]
            rhs = jnp.concatenate([jnp.concatenate([lines[a], lines[a + 1]], axis=1) for a in range(3)], axis=0)
            got = jnp.dot(w[pl.ds(lo * chans, (hi - lo) * chans)], rhs, preferred_element_type=F32)

            def store():
                for tap in taps:
                    n = f - tap
                    for j in range(2):
                        mine = got[(tap - lo) * chans:(tap - lo + 1) * chans, j * cols:(j + 1) * cols]
                        total = mine + (start_of(n, r + j) if tap == 2 else acc[n, r + j])
                        if tap == 0 and done is not None:
                            done(n, r + j, total)
                        else:
                            acc[n, r + j] = total
            return [store]
        return step

    mids = frames + 2

    def conv_a(f):
        return conv(x1, w1, acc1, f, mids - 1, lambda n, r: vecs[2], None)

    def finished(n, r, total):
        out[n, r] = total.astype(BF16)

    def conv_b(f):
        return conv(x2, w2, acc2, f, frames - 1, lambda n, r: ups[n, r + 2].astype(F32) + vecs[4], finished)

    def second(n, r):
        act = norm_act(acc1[n, r], vecs[3])
        keep = row_keep(r, 1, rows + 1)
        if n < 2:
            keep = keep * past_keep
        return [put(x2, n, r, act * keep)]

    def second_two(n):
        return lambda p: second(n, 2 * p) + second(n, 2 * p + 1)

    newest = 2 * frames - 1
    def lone(pairs):
        for pair in pairs:
            for store in expand(newest)(pair):
                store()

    lone((1, 2))
    pl.when(has_down)(to_up.wait_recv)
    pl.when(has_up)(to_down.wait_recv)

    def relay(f):
        @pl.when(has_prev)
        def _():
            far[f].wait_recv()
            pl.when(has_up)(hop_up[f].start)
            pl.when(has_down)(hop_down[f].start)

    def landed(f):
        @pl.when(has_prev)
        def _():
            pl.when(has_down)(hop_up[f].wait_recv)
            pl.when(has_up)(hop_down[f].wait_recv)

    lone((0, 3))
    wide_pairs = (rows + 2) // 2
    for f in reversed(range(2 * frames)):
        if 0 < f <= frames:
            landed(f - 1)
        level(f, f - 1 if f > 0 else None)
        if f >= frames:
            relay(f - frames)
        ready = f + 1
        if ready < mids:
            run(wide_pairs, second_two(ready), conv_a(f))
        else:
            run(wide_pairs, conv_a(f))
    run(wide_pairs, second_two(0))
    for f in reversed(range(mids)):
        run(rows // 2, conv_b(f))

    pl.when(has_up)(to_up.wait_send)
    pl.when(has_down)(to_down.wait_send)
    for f in range(frames):
        pl.when(has_next)(far[f].wait_send)
        pl.when(jnp.logical_and(has_prev, has_up))(hop_up[f].wait_send)
        pl.when(jnp.logical_and(has_prev, has_down))(hop_down[f].wait_send)


def shards(slabs, tiles, coarse, up_weight, up_bias, gain_one, conv_one, bias_one, gain_two, conv_two, bias_two):
    deep, frames, lines, half = coarse.shape
    chans = up_weight.shape[2]
    rows, cols = 2 * lines, 2 * half
    packed = coarse.transpose(1, 2, 0, 3).reshape(frames, lines // 2, 2, deep, half)
    packed = packed.transpose(0, 1, 3, 2, 4).reshape(frames, lines // 2, deep, cols)
    row = lambda vec: vec.reshape(1, chans)
    vmem = pl.BlockSpec(memory_space=pltpu.VMEM)
    got = pl.pallas_call(
        functools.partial(body, slabs, tiles),
        out_shape=jax.ShapeDtypeStruct((frames, rows, chans, cols), BF16),
        in_specs=[vmem] * 9,
        out_specs=vmem,
        scratch_shapes=[
            pltpu.VMEM((2 * frames, 4, deep, cols), BF16),
            pltpu.VMEM((4 * chans, 3 * deep), BF16),
            pltpu.VMEM((3 * chans, 9 * chans), BF16),
            pltpu.VMEM((3 * chans, 9 * chans), BF16),
            pltpu.VMEM((5, chans, cols), F32),
            pltpu.VMEM((cols, 2 * cols), BF16),
            pltpu.VMEM((2, 8, 4 * chans, cols), F32),
            pltpu.VMEM((frames, rows + 4, chans, cols), BF16),
            pltpu.VMEM((2 * frames, rows + 4, 3 * chans, cols), BF16),
            pltpu.VMEM((frames + 2, rows + 2, chans, cols), F32),
            pltpu.VMEM((frames + 2, rows + 2, 3 * chans, cols), BF16),
            pltpu.VMEM((frames, rows, chans, cols), F32),
            pltpu.SemaphoreType.DMA((2,)),
            pltpu.SemaphoreType.DMA((2,)),
            pltpu.SemaphoreType.DMA((frames,)),
            pltpu.SemaphoreType.DMA((frames,)),
            pltpu.SemaphoreType.DMA((frames, 2)),
            pltpu.SemaphoreType.DMA((frames, 2)),
        ],
        compiler_params=pltpu.CompilerParams(collective_id=0, has_side_effects=True, vmem_limit_bytes=48 * 2**20),
    )(packed, up_weight, conv_one, conv_two, row(up_bias), row(gain_one), row(bias_one), row(gain_two), row(bias_two))
    return got.transpose(2, 0, 1, 3)


def solution(mesh):
    return jax.shard_map(
        functools.partial(shards, mesh.shape["slab"], mesh.shape["tile"]),
        mesh=mesh,
        in_specs=(P(None, "slab", "tile", None), P(), P(), P(), P(), P(), P(), P(), P()),
        out_specs=P(None, "slab", "tile", None),
        check_vma=False,
    )
```
